32 devices in a mesh: cls: 8 (over z, x), img: 4 (over y, core).
Axes of the slice: x: 2, y: 2, z: 4, core: 2. Of those that a mesh axis runs over, the one named last changes fastest.
Arguments:
- images: bfloat16 [512, 9216], P(('cls', 'img')), may hold values from -9 to 9
- ctf: bfloat16 [512, 4608], P(('cls', 'img')), may hold values from -1 to 1
- classes: int32 [512, 4], P(('cls', 'img')), may hold values from 0 to 55, as said below
- class_place: int32 [56], replicated, may hold values from 0 to 55, as said below
- references: bfloat16 [56, 9216], P('cls'), may hold values from -3 to 3
- sigma2: float32 [64], replicated, may hold values from 0.05 to 4, as said below
Outputs:
- new_references: float32 [56, 9216], P('cls', 'img')
The draws below stay inside these ranges and needn't reach their ends.
Inputs may be any that keep to these rules, and one draw needn't show every extreme that they name: Each particle names 4 different classes whose table rows class_place[k] lie in 4 different groups of 7 consecutive table rows. Among the 16 particles of one device (aligned blocks of 16 rows) at most 8 list entries fall in one group, and in every block some group receives exactly 8. A permutation: class k is held in table row class_place[k]. `sigma2`: positive noise powers.
All inputs are finite; a program needn't handle non-finite values.
Results may differ from the reference program's by a relative error of at most 0.0018.
Values may be sent and summed in bfloat16 or wider, within the bound.
A program may use at most 128 MiB of HBM per device.

```python
import math
import jax
import jax.numpy as jnp
from jax import lax

S = 64
NA = 72
TOP = 4
K_DEV = 7
P_DEV = 16
CAP = 8
K = 56
NP = 512


def routing_tables(key):
    owners = K // K_DEV
    blocks = NP // P_DEV
    groups = blocks // owners
    pick_count = TOP * P_DEV
    placement = jax.random.permutation(jax.random.fold_in(key, 7), K).astype(jnp.int32)
    inverse = jnp.zeros((K,), jnp.int32).at[placement].set(jnp.arange(K, dtype=jnp.int32))
    hot_group = jax.random.randint(jax.random.fold_in(key, 8), (groups,), 0, owners)
    hot_block = hot_group[jnp.arange(blocks) % groups]
    block_keys = jax.random.split(jax.random.fold_in(key, 9), blocks)
    remaining = pick_count - CAP
    even_load = remaining // (owners - 1)
    extra_load = remaining % (owners - 1)
    pair_count = max((owners - 1) // 2, 1)

    def one_block(block_key, hot_owner):
        key_rank, key_move, key_order, key_offset, key_rows = jax.random.split(block_key, 5)
        ordering = jax.random.permutation(key_rank, owners)
        ranking = jnp.zeros((owners,), jnp.int32).at[ordering].set(jnp.arange(owners, dtype=jnp.int32))
        other_rank = ranking - (ranking > ranking[hot_owner]).astype(jnp.int32)
        loads = even_load + (other_rank < extra_load).astype(jnp.int32)
        pair_index = jnp.arange(pair_count, dtype=jnp.int32)
        low_load = even_load + (2 * pair_index < extra_load).astype(jnp.int32)
        high_load = even_load + (2 * pair_index + 1 < extra_load).astype(jnp.int32)
        move_limit = jnp.maximum(jnp.minimum(low_load, CAP - high_load), 0)
        shifted_by = jax.random.randint(key_move, (pair_count,), 0, move_limit + 1)
        paired = other_rank < 2 * ((owners - 1) // 2)
        partner = jnp.minimum(other_rank // 2, pair_count - 1)
        change = jnp.where(other_rank % 2 == 0, -shifted_by[partner], shifted_by[partner])
        loads = jnp.where(paired, loads + change, loads)
        loads = jnp.where(jnp.arange(owners) == hot_owner, CAP, loads).astype(jnp.int32)
        sequence = jax.random.permutation(key_order, owners)
        ordered = loads[sequence]
        run_end = jnp.cumsum(ordered)
        starts = run_end - ordered
        pick_slot = jnp.arange(pick_count, dtype=jnp.int32)
        position = jnp.sum((pick_slot[:, None] >= run_end[None, :]).astype(jnp.int32), axis=1)
        owner_id = sequence[position]
        within = pick_slot - starts[position]
        offset = jax.random.randint(key_offset, (owners,), 0, K_DEV)
        table_row = owner_id * K_DEV + (offset[owner_id] + within) % K_DEV
        chosen = inverse[table_row].reshape(TOP, P_DEV).T
        return chosen[jax.random.permutation(key_rows, P_DEV)]
    class_lists = jax.vmap(one_block)(block_keys, hot_block)
    return (placement, class_lists.reshape(NP, TOP).astype(jnp.int32))


def bright_setup(key):
    bright_count = max(1, K // 32)
    bright_rows = jax.random.permutation(jax.random.fold_in(key, 21), K)[:bright_count]
    is_bright = jnp.zeros((K,), jnp.bool_).at[bright_rows].set(True)
    strength = jax.random.uniform(jax.random.fold_in(key, 22), (K,), jnp.float32, 1.5, 3.0)
    amplitude = jnp.where(is_bright, jnp.sqrt(536.0 * strength / (S * NA)), 0.05)
    return (is_bright, amplitude)


def draw_classes(key, part):
    return routing_tables(key)[1]


def draw_class_place(key, part):
    return routing_tables(key)[0]


def draw_sigma2(key, part):
    spread = jax.random.uniform(key, (S,), jnp.float32, math.log(0.5), math.log(4.0))
    noise_power = jnp.exp(spread)
    return noise_power.astype(jnp.float32)


def draw_references(key, part):
    is_bright, amplitude = bright_setup(key)
    inner = jax.random.fold_in(key, 23)
    base = jax.random.truncated_normal(inner, -3.0, 3.0, (K, S * 2 * NA), jnp.float32)
    return (base * amplitude[:, None]).astype(jnp.bfloat16)


def draw_ctf(key, part):
    return jax.random.uniform(jax.random.fold_in(key, 24), (NP, S * NA), jnp.float32, -1.0, 1.0).astype(jnp.bfloat16)


def draw_images(key, part):
    placement, class_lists = routing_tables(key)
    is_bright, amplitude = bright_setup(key)
    inner = jax.random.fold_in(key, 25)
    noise = jax.random.truncated_normal(inner, -6.0, 6.0, (NP, S, 2, NA), jnp.float32)
    rows = placement[class_lists]
    hit = is_bright[rows]
    has_bright = jnp.any(hit, axis=1)
    first = jnp.argmax(hit.astype(jnp.int32), axis=1)
    row_pick = jnp.take_along_axis(rows, first[:, None], axis=1)[:, 0]
    table = draw_references(key, part).reshape(K, S, 2, NA)
    picked = table[row_pick]
    turn_by = jax.random.randint(jax.random.fold_in(key, 26), (NP,), 0, NA)
    index = (jnp.arange(NA, dtype=jnp.int32)[None, :] - turn_by[:, None]) % NA
    turned = jnp.take_along_axis(picked, index[:, None, None, :], axis=3)
    ctf_values = draw_ctf(key, part).reshape(NP, S, NA)
    aligned = ctf_values[:, :, None, :] * turned
    images = noise + jnp.where(has_bright[:, None, None, None], aligned, 0.0)
    return images.reshape(NP, S * 2 * NA).astype(jnp.bfloat16)


def setup_inputs(seed: int = 0) -> dict:
    streams_of = jax.random.split(jax.random.key(seed), 7)
    return {
        "images": draw_images(jax.random.fold_in(streams_of[6], 71), 0),
        "ctf": draw_ctf(jax.random.fold_in(streams_of[6], 71), 0),
        "classes": draw_classes(jax.random.fold_in(streams_of[6], 71), 0),
        "class_place": draw_class_place(jax.random.fold_in(streams_of[6], 71), 0),
        "references": draw_references(jax.random.fold_in(streams_of[6], 71), 0),
        "sigma2": draw_sigma2(jax.random.fold_in(streams_of[6], 71), 0),
    }


def reference(images, ctf, classes, class_place, references, sigma2):
    shells = sigma2.shape[0]
    angles = ctf.shape[1] // shells
    class_total = class_place.shape[0]
    ref_table = references.astype(jnp.float32).reshape(class_total, shells, 2, angles)
    ref_power = jnp.sum(ref_table * ref_table, axis=2).astype(jnp.bfloat16)
    ref_power = lax.optimization_barrier(ref_power).astype(jnp.float32)
    table_hat = jnp.fft.rfft(ref_table, axis=-1)
    power_hat = jnp.fft.rfft(ref_power, axis=-1)
    table_rows = class_place[classes].astype(jnp.int32)
    inverse_sigma = 1.0 / sigma2
    block_count = 32
    block_rows = images.shape[0] // block_count
    num_zero = jnp.zeros(table_hat.shape, table_hat.dtype)
    den_zero = jnp.zeros(power_hat.shape, power_hat.dtype)

    def advance(carry, block_data):
        num_hat, den_hat = carry
        image_block, ctf_block, rows_block = block_data
        scaling = ctf_block.astype(jnp.float32).reshape(block_rows, shells, angles) * inverse_sigma[None, :, None]
        weighted = (image_block.astype(jnp.float32).reshape(block_rows, shells, 2, angles) * scaling[:, :, None, :]).astype(jnp.bfloat16)
        ctf_power = (ctf_block.astype(jnp.float32).reshape(block_rows, shells, angles) * scaling).astype(jnp.bfloat16)
        weighted, ctf_power = lax.optimization_barrier((weighted, ctf_power))
        weighted_hat = jnp.fft.rfft(weighted.astype(jnp.float32), axis=-1)
        ctf_hat = jnp.fft.rfft(ctf_power.astype(jnp.float32), axis=-1)
        ref_rows = table_hat[rows_block]
        pow_rows = power_hat[rows_block]
        cross_term = jnp.fft.irfft(jnp.sum(weighted_hat[:, None] * jnp.conj(ref_rows), axis=(2, 3)), n=angles, axis=-1)
        quad_term = jnp.fft.irfft(jnp.sum(ctf_hat[:, None] * jnp.conj(pow_rows), axis=2), n=angles, axis=-1)
        logits = cross_term - 0.5 * quad_term
        highest = jnp.max(logits, axis=(1, 2), keepdims=True)
        exponent = jnp.exp(logits - highest)
        posterior = (exponent / jnp.sum(exponent, axis=(1, 2), keepdims=True)).astype(jnp.bfloat16)
        posterior = lax.optimization_barrier(posterior).astype(jnp.float32)
        post_hat = jnp.conj(jnp.fft.rfft(posterior, axis=-1))
        num_hat = num_hat.at[rows_block].add(weighted_hat[:, None] * post_hat[:, :, None, None, :])
        den_hat = den_hat.at[rows_block].add(ctf_hat[:, None] * post_hat[:, :, None, :])
        return (num_hat, den_hat), None

    block_data = (images.reshape(block_count, block_rows, -1), ctf.reshape(block_count, block_rows, -1), table_rows.reshape(block_count, block_rows, -1))
    (num_hat, den_hat), unused = lax.scan(advance, (num_zero, den_zero), block_data)
    numerator = jnp.fft.irfft(num_hat, n=angles, axis=-1)
    denominator = jnp.fft.irfft(den_hat, n=angles, axis=-1)
    updated = numerator / (denominator[:, :, None, :] + 1.0)
    return updated.reshape(class_total, -1)
```

```python
import functools

import jax
import jax.numpy as jnp
import numpy as np
from jax import lax
from jax.experimental import pallas as pl
from jax.experimental.pallas import tpu as pltpu
from jax.sharding import PartitionSpec as P

MESH = pl.DeviceIdType.MESH
VMEM = pltpu.VMEM
F32 = jnp.float32
BF16 = jnp.bfloat16
LANES = 128
IMAG = 64
LAST = (((1,), (1,)), ((), ()))


def specs(count, space=pltpu.VMEM):
    return [pl.BlockSpec(memory_space=space)] * count


def round_up(x, step):
    return -(-x // step) * step


def waves(angles):
    turns = angles // 2 + 1
    step = 2 * np.pi * np.outer(np.arange(angles), np.arange(turns)) / angles
    cos = np.zeros((LANES, IMAG))
    sin = np.zeros((LANES, IMAG))
    cos[:angles, :turns] = np.cos(step)
    sin[:angles, :turns] = np.sin(step)
    share = np.zeros((IMAG,))
    share[:turns] = 2.0 / angles
    share[0] = 1.0 / angles
    if angles % 2 == 0:
        share[turns - 1] = 1.0 / angles
    back = np.concatenate([cos * share, -sin * share], axis=1)
    return cos, sin, back


def halves(x):
    high = np.asarray(x, dtype=BF16)
    low = np.asarray(x - high.astype(np.float64), dtype=BF16)
    return high, low


def paired(*forms):
    return np.concatenate([part for form in forms for part in halves(form)], axis=1)


def greet(groups):
    barrier = pltpu.get_barrier_semaphore()
    total = 0
    for axis, size in groups:
        me = lax.axis_index(axis)
        for step in range(1, size):
            peer = lax.rem(me + step, size)
            pl.semaphore_signal(barrier, inc=1, device_id={axis: peer}, device_id_type=MESH)
            total += 1
    pl.semaphore_wait(barrier, total)


def remote(src, dst, send, recv, axis, peer):
    return pltpu.make_async_remote_copy(
        src_ref=src,
        dst_ref=dst,
        send_sem=send,
        recv_sem=recv,
        device_id={axis: peer},
        device_id_type=MESH,
    )


def lane_of(shape):
    return lax.broadcasted_iota(jnp.int32, shape, len(shape) - 1)


def roll(x, shift):
    return pltpu.roll(x, shift % LANES, x.ndim - 1)


def piece(tiles, start, count):
    tile, offset = divmod(start, LANES)
    if offset == 0:
        return tiles[tile]
    first = roll(tiles[tile], -offset)
    if offset + count <= LANES:
        return first
    return jnp.where(lane_of(first.shape) < LANES - offset, first, roll(tiles[tile + 1], -offset))


def tiles_of(x):
    return [x[:, begin : begin + LANES].astype(F32) for begin in range(0, x.shape[1], LANES)]


def group_of(x, top, combine):
    row = lax.broadcasted_iota(jnp.int32, x.shape, 0)
    count = x.shape[0]
    step = 1
    while step < top:
        swapped = jnp.where(
            (row // step) % 2 == 0, pltpu.roll(x, count - step, 0), pltpu.roll(x, step, 0)
        )
        x = combine(x, swapped)
        step *= 2
    return x


def score_kernel(
    dims, place_ref, sigma_ref, w_ref, c_ref, r_ref, t_ref, fw_ref, fr_ref, back_ref,
    what, post, tall,
    wall, call, rall, rows_ref, real, imag, parts, landed,
    own_sem, ws, wr, cs, cr, rs, rr, ts, tr, ls, lr, ps, pr,
):
    fellows, particles, owners, per_owner, top, angles, half = dims
    rows = 3 * half
    wide = wall.shape[2]
    thin = call.shape[2]
    entries = particles * top
    my_owner = lax.axis_index("cls")
    my_fellow = lax.axis_index("img")
    greet((("cls", owners), ("img", fellows)))

    def columns(ref, fellow, count):
        return ref.at[:, pl.ds(pl.multiple_of(fellow * count, LANES), count)]

    mine = columns(r_ref, my_fellow, wide)
    row_copies = []
    ref_copies = []
    image_copies = []
    for step in range(1, fellows):
        peer = lax.rem(my_fellow + step, fellows)
        row_copies.append(remote(t_ref, tall.at[my_fellow], ts.at[step], tr.at[step], "img", peer))
        image_copies.append(
            remote(
                columns(c_ref, peer, thin), call.at[my_fellow], cs.at[step], cr.at[step], "img", peer
            )
        )
        image_copies.append(
            remote(
                columns(w_ref, peer, wide), wall.at[my_fellow], ws.at[step], wr.at[step], "img", peer
            )
        )
    for step in range(1, owners):
        peer = lax.rem(my_owner + step, owners)
        ref_copies.append(remote(mine, rall.at[my_owner], rs.at[step], rr.at[step], "cls", peer))
    for copy in row_copies + ref_copies + image_copies:
        copy.start()
    own_copies = [
        pltpu.make_async_copy(t_ref, tall.at[my_fellow], own_sem.at[0]),
        pltpu.make_async_copy(columns(c_ref, my_fellow, thin), call.at[my_fellow], own_sem.at[1]),
        pltpu.make_async_copy(columns(w_ref, my_fellow, wide), wall.at[my_fellow], own_sem.at[2]),
        pltpu.make_async_copy(mine, rall.at[my_owner], own_sem.at[3]),
    ]
    for copy in own_copies:
        copy.start()

    inverses = [
        1.0 / jnp.full((particles, LANES), sigma_ref[my_fellow * half + s], F32) for s in range(half)
    ]

    flat_real = real.reshape(owners * per_owner * rows, LANES)
    flat_imag = imag.reshape(owners * per_owner * rows, LANES)

    def transform(blocks, table):
        x = jnp.concatenate(blocks, axis=0).astype(BF16)
        return jnp.dot(x, table, preferred_element_type=F32)

    def place(fellow):
        num = tiles_of(wall[fellow])
        den = tiles_of(call[fellow])
        weighted = []
        power = []
        for s in range(half):
            ctf = piece(den, s * angles, angles)
            scale = ctf * inverses[s]
            power.append(ctf * scale)
            for p in range(2):
                weighted.append(piece(num, (2 * s + p) * angles, angles) * scale)
        hat = transform(weighted + power, fw_ref[...])
        hat = hat[:, :LANES] + hat[:, LANES:]
        for row in range(rows):
            what[pl.ds(fellow * (particles * rows) + row, particles, stride=rows)] = hat[
                row * particles : (row + 1) * particles
            ]

    def tabulate(owner):
        ref = tiles_of(rall[owner])
        given = []
        power = []
        for s in range(half):
            pair = [piece(ref, (2 * s + p) * angles, angles) for p in range(2)]
            given += pair
            squares = pair[0] * pair[0] + pair[1] * pair[1]
            power.append(squares.astype(BF16).astype(F32) * -0.5)
        tall_rows = round_up(per_owner, 8)
        blocks = [
            jnp.concatenate([x, jnp.zeros((tall_rows - per_owner, LANES), F32)], axis=0)
            for x in given + power
        ]
        hat = transform(blocks, fr_ref[...])
        for row in range(rows):
            at = pl.ds(owner * (per_owner * rows) + row, per_owner, stride=rows)
            block = hat[row * tall_rows : row * tall_rows + per_owner]
            flat_real[at] = block[:, :LANES] + block[:, LANES : 2 * LANES]
            flat_imag[at] = block[:, 2 * LANES : 3 * LANES] + block[:, 3 * LANES :]

    for copy in own_copies:
        copy.wait()
    place(my_fellow)
    tabulate(my_owner)
    for copy in row_copies:
        copy.wait_recv()
    to_smem = pltpu.make_async_copy(tall, rows_ref, own_sem.at[4])
    to_smem.start()
    for step in range(1, max(owners, fellows)):
        if step < fellows:
            image_copies[2 * step - 2].wait_recv()
            image_copies[2 * step - 1].wait_recv()
            place(lax.rem(my_fellow + fellows - step, fellows))
        if step < owners:
            ref_copies[step - 1].wait_recv()
            tabulate(lax.rem(my_owner + owners - step, owners))
    to_smem.wait()

    batch = 4

    def score(fellow):
        def some(b, carry):
            sums = []
            for k in range(batch):
                i = b * batch + k
                base = pl.multiple_of((fellow * particles + i) * rows, 8)
                held = what[pl.ds(base, rows)]
                for j in range(top):
                    row = place_ref[rows_ref[fellow, j, i]]
                    first = held * real[row]
                    second = held * imag[row]
                    first = jnp.sum(first.reshape(rows // 8, 8, LANES), axis=0)
                    second = jnp.sum(second.reshape(rows // 8, 8, LANES), axis=0)
                    sums.append(jnp.sum(first + roll(second, IMAG), axis=0, keepdims=True))
            count = batch * top
            parts[fellow, pl.ds(pl.multiple_of(b * count, count), count)] = jnp.concatenate(
                sums, axis=0
            )
            return carry

        lax.fori_loop(0, particles // batch, some, 0)

    part_copies = []
    for step in range(1, fellows):
        peer = lax.rem(my_fellow + fellows - step, fellows)
        score(peer)
        copy = remote(
            parts.at[peer], landed.at[step - 1], ls.at[step], lr.at[step], "img", peer
        )
        copy.start()
        part_copies.append(copy)
    score(my_fellow)
    total = parts[my_fellow]
    for step in range(1, fellows):
        part_copies[step - 1].wait_recv()
        total = total + landed[step - 1]
    logits = jnp.dot(
        total, back_ref[...], precision=lax.Precision.HIGHEST, preferred_element_type=F32
    )
    inside = lane_of(logits.shape) < angles
    highest = jnp.max(jnp.where(inside, logits, -jnp.inf), axis=1, keepdims=True)
    highest = group_of(jnp.broadcast_to(highest, logits.shape), top, jnp.maximum)
    exponent = jnp.where(inside, jnp.exp(logits - highest), 0.0)
    summed = jnp.sum(exponent, axis=1, keepdims=True)
    summed = group_of(jnp.broadcast_to(summed, logits.shape), top, jnp.add)
    post[my_fellow] = (exponent / summed).astype(BF16)
    post_copies = []
    for step in range(1, fellows):
        peer = lax.rem(my_fellow + step, fellows)
        at = post.at[my_fellow]
        copy = remote(at, at, ps.at[step], pr.at[step], "img", peer)
        copy.start()
        post_copies.append(copy)
    for copy in row_copies + ref_copies + image_copies + part_copies:
        copy.wait_send()
    for copy in post_copies:
        copy.wait()


def total_kernel(dims, place_ref, rows_ref, what, post, fp_ref, acc, real, imag):
    fellows, particles, owners, per_owner, top, angles, half = dims
    rows = 3 * half
    hat = jnp.dot(post[...].reshape(-1, LANES), fp_ref[...], preferred_element_type=F32)
    real[...] = hat[:, :LANES] + hat[:, LANES : 2 * LANES]
    imag[...] = hat[:, 2 * LANES : 3 * LANES] + hat[:, 3 * LANES :]
    acc[...] = jnp.zeros_like(acc)
    batch = 4

    def one(fellow, i):
        at = fellow * particles + i
        held = what[pl.ds(pl.multiple_of(at * rows, 8), rows)]
        swapped = roll(held, IMAG)
        spots = [
            pl.ds(pl.multiple_of(place_ref[rows_ref[fellow, j, i]] * rows, 8), rows)
            for j in range(top)
        ]
        before = [acc[spot] for spot in spots]
        for j in range(top):
            e = at * top + j
            acc[spots[j]] = before[j] + held * real[pl.ds(e, 1)] + swapped * imag[pl.ds(e, 1)]

    def some(b, carry):
        for k in range(batch):
            one(b // (particles // batch), lax.rem(b, particles // batch) * batch + k)
        return carry

    lax.fori_loop(0, fellows * particles // batch, some, 0)


def gather_kernel(dims, acc, high_ref, low_ref, out_ref, outbox, landed, flat, send, recv):
    fellows, particles, owners, per_owner, top, angles, half = dims
    rows = 3 * half
    lanes = outbox.shape[2]
    me = lax.axis_index("cls")
    greet((("cls", owners),))

    def sums(owner):
        x = acc[pl.ds(pl.multiple_of(owner * (per_owner * rows), 8), lanes)]
        high = x.astype(BF16)
        low = (x - high.astype(F32)).astype(BF16)

        def turned(a, b):
            return lax.dot_general(a, b, LAST, preferred_element_type=F32)

        return turned(high_ref[...], high) + (
            turned(high_ref[...], low) + turned(low_ref[...], high)
        )

    copies = []
    for step in range(1, owners):
        peer = lax.rem(me + step, owners)
        outbox[peer] = sums(peer)[:angles].astype(BF16)
        copy = remote(
            outbox.at[peer], landed.at[step - 1], send.at[step], recv.at[step], "cls", peer
        )
        copy.start()
        copies.append(copy)
    total = sums(me)[:angles]
    for step in range(1, owners):
        copies[step - 1].wait_recv()
        total = total + landed[step - 1].astype(F32)
    total = jnp.concatenate([total, jnp.zeros((LANES - angles, lanes), F32)], axis=0)
    for begin in range(0, lanes, LANES):
        flat[begin : begin + LANES] = total[:, begin : begin + LANES].T
    count = out_ref.shape[1] // LANES
    tiles = [jnp.zeros((per_owner, LANES), F32) for _ in range(count)]
    lane = lane_of((per_owner, LANES))
    for s in range(half):
        den = flat[pl.ds(2 * half + s, per_owner, stride=rows)] + 1.0
        for p in range(2):
            new = flat[pl.ds(2 * s + p, per_owner, stride=rows)] / den
            tile, offset = divmod((2 * s + p) * angles, LANES)
            new = roll(new, offset) if offset else new
            within = (lane >= offset) & (lane < offset + angles)
            tiles[tile] = jnp.where(within, new, tiles[tile])
            if offset + angles > LANES:
                tiles[tile + 1] = jnp.where(lane < offset + angles - LANES, new, tiles[tile + 1])
    for tile, value in enumerate(tiles):
        out_ref[:, tile * LANES : (tile + 1) * LANES] = value
    for copy in copies:
        copy.wait_send()


def spaced(x, fellows):
    count = x.shape[1] // fellows
    wanted = round_up(count, LANES)
    if wanted == count:
        return x, count
    x = jnp.pad(x.reshape(x.shape[0], fellows, count), ((0, 0), (0, 0), (0, wanted - count)))
    return x.reshape(x.shape[0], fellows * wanted), wanted


def on_device(images, ctf, classes, class_place, references, sigma2):
    shells = sigma2.shape[0]
    angles = ctf.shape[1] // shells
    particles = images.shape[0]
    per_owner = references.shape[0]
    top = classes.shape[1]
    owners = lax.axis_size("cls")
    fellows = lax.axis_size("img")
    half = shells // fellows
    rows = 3 * half
    dims = (fellows, particles, owners, per_owner, top, angles, half)
    everyone = fellows * particles
    total = owners * per_owner
    lanes = round_up(per_owner * rows, LANES)
    acc_rows = round_up((total - per_owner) * rows + lanes, 8)

    images, wide = spaced(images, fellows)
    ctf, thin = spaced(ctf, fellows)
    references, _ = spaced(references, fellows)

    cos, sin, back = waves(angles)
    both = np.concatenate([cos, cos], axis=1)
    forward = jnp.asarray(paired(np.concatenate([cos, -sin], axis=1)))
    of_refs = jnp.asarray(paired(both, np.concatenate([sin, -sin], axis=1)))
    of_post = jnp.asarray(paired(both, np.concatenate([-sin, sin], axis=1)))
    back_high, back_low = halves(back[: round_up(angles, 16)])
    smem = pl.BlockSpec(memory_space=pltpu.SMEM)
    dma = pltpu.SemaphoreType.DMA
    what, post, tall = pl.pallas_call(
        functools.partial(score_kernel, dims),
        out_shape=(
            jax.ShapeDtypeStruct((everyone * rows, LANES), F32),
            jax.ShapeDtypeStruct((fellows, particles * top, LANES), BF16),
            jax.ShapeDtypeStruct((fellows, top, particles), jnp.int32),
        ),
        in_specs=[smem, smem] + specs(4, pl.ANY) + specs(3),
        out_specs=tuple(specs(3)),
        scratch_shapes=[
            VMEM((fellows, particles, wide), BF16),
            VMEM((fellows, particles, thin), BF16),
            VMEM((owners, per_owner, wide), BF16),
            pltpu.SMEM((fellows, top, particles), jnp.int32),
            VMEM((total, rows, LANES), F32),
            VMEM((total, rows, LANES), F32),
            VMEM((fellows, particles * top, LANES), F32),
            VMEM((fellows - 1, particles * top, LANES), F32),
            dma((5,)),
            dma((fellows,)),
            dma((fellows,)),
            dma((fellows,)),
            dma((fellows,)),
            dma((owners,)),
            dma((owners,)),
            dma((fellows,)),
            dma((fellows,)),
            dma((fellows,)),
            dma((fellows,)),
            dma((fellows,)),
            dma((fellows,)),
        ],
        compiler_params=pltpu.CompilerParams(collective_id=0, has_side_effects=True),
    )(
        class_place, sigma2, images, ctf, references, classes.T,
        forward, of_refs, jnp.asarray(back.T, F32),
    )
    acc = pl.pallas_call(
        functools.partial(total_kernel, dims),
        out_shape=jax.ShapeDtypeStruct((acc_rows, LANES), F32),
        in_specs=[smem, smem] + specs(3),
        out_specs=specs(1)[0],
        scratch_shapes=[VMEM((everyone * top, LANES), F32)] * 2,
    )(class_place, tall, what, post, of_post)
    return pl.pallas_call(
        functools.partial(gather_kernel, dims),
        out_shape=jax.ShapeDtypeStruct((per_owner, 2 * half * angles), F32),
        in_specs=specs(3),
        out_specs=specs(1)[0],
        scratch_shapes=[
            VMEM((owners, angles, lanes), BF16),
            VMEM((owners - 1, angles, lanes), BF16),
            VMEM((lanes, LANES), F32),
            dma((owners,)),
            dma((owners,)),
        ],
        compiler_params=pltpu.CompilerParams(collective_id=2, has_side_effects=True),
    )(acc, jnp.asarray(back_high), jnp.asarray(back_low))


def solution(mesh):
    in_specs = (
        P(("cls", "img"), None),
        P(("cls", "img"), None),
        P(("cls", "img"), None),
        P(),
        P("cls", None),
        P(),
    )
    out_specs = P("cls", "img")
    return jax.shard_map(
        on_device, mesh=mesh, in_specs=in_specs, out_specs=out_specs, check_vma=False
    )
```

```python
import functools

import jax
import jax.numpy as jnp
import numpy as np
from jax import lax
from jax.experimental import pallas as pl
from jax.experimental.pallas import tpu as pltpu
from jax.sharding import PartitionSpec as P

MESH = pl.DeviceIdType.MESH
VMEM = pltpu.VMEM
F32 = jnp.float32
BF16 = jnp.bfloat16
LANES = 128
IMAG = 64
LIMIT = 20 * 2**20
WIDE = 61500000
LAST = (((1,), (1,)), ((), ()))


def specs(count, space=pltpu.VMEM):
    return [pl.BlockSpec(memory_space=space)] * count


def round_up(x, step):
    return -(-x // step) * step


def waves(angles):
    turns = angles // 2 + 1
    step = 2 * np.pi * np.outer(np.arange(angles), np.arange(turns)) / angles
    cos = np.zeros((LANES, IMAG))
    sin = np.zeros((LANES, IMAG))
    cos[:angles, :turns] = np.cos(step)
    sin[:angles, :turns] = np.sin(step)
    share = np.zeros((IMAG,))
    share[:turns] = 2.0 / angles
    share[0] = 1.0 / angles
    if angles % 2 == 0:
        share[turns - 1] = 1.0 / angles
    back = np.concatenate([cos * share, -sin * share], axis=1)
    return cos, sin, back


def halves(x):
    high = np.asarray(x, dtype=BF16)
    low = np.asarray(x - high.astype(np.float64), dtype=BF16)
    return high, low


def paired(*forms):
    return np.concatenate([part for form in forms for part in halves(form)], axis=1)


def hail(groups):
    barrier = pltpu.get_barrier_semaphore()
    total = 0
    for axis, size in groups:
        me = lax.axis_index(axis)
        for step in range(1, size):
            peer = lax.rem(me + step, size)
            pl.semaphore_signal(barrier, inc=1, device_id={axis: peer}, device_id_type=MESH)
            total += 1
    return lambda: pl.semaphore_wait(barrier, total)


def remote(src, dst, send, recv, axis, peer):
    return pltpu.make_async_remote_copy(
        src_ref=src,
        dst_ref=dst,
        send_sem=send,
        recv_sem=recv,
        device_id={axis: peer},
        device_id_type=MESH,
    )


def lane_of(shape):
    return lax.broadcasted_iota(jnp.int32, shape, len(shape) - 1)


def roll(x, shift):
    return pltpu.roll(x, shift % LANES, x.ndim - 1)


def piece(tiles, start, count):
    tile, offset = divmod(start, LANES)
    if offset == 0:
        return tiles[tile]
    first = roll(tiles[tile], -offset)
    if offset + count <= LANES:
        return first
    return jnp.where(lane_of(first.shape) < LANES - offset, first, roll(tiles[tile + 1], -offset))


def tiles_of(x):
    return [x[:, begin : begin + LANES].astype(F32) for begin in range(0, x.shape[1], LANES)]


def group_of(x, top, combine):
    row = lax.broadcasted_iota(jnp.int32, x.shape, 0)
    count = x.shape[0]
    step = 1
    while step < top:
        swapped = jnp.where(
            (row // step) % 2 == 0, pltpu.roll(x, count - step, 0), pltpu.roll(x, step, 0)
        )
        x = combine(x, swapped)
        step *= 2
    return x


def score_kernel(
    dims, place_hbm, sigma_hbm, w_ref, c_ref, r_ref, t_ref, fw_hbm, fr_hbm, fp_hbm, back_hbm,
    what, post_real, post_imag, tall, place_out,
    place_ref, sigma_ref, fw_ref, fr_ref, fp_ref, back_ref, post,
    wall, call, rall, rows_ref, real, imag, parts, landed,
    own_sem, ws, wr, cs, cr, rs, rr, ts, tr, ls, lr, ps, pr,
):
    fellows, particles, owners, per_owner, top, angles, half = dims
    rows = 3 * half
    wide = wall.shape[2]
    thin = call.shape[2]
    entries = particles * top
    my_owner = lax.axis_index("cls")
    my_fellow = lax.axis_index("img")
    arrive = hail((("cls", owners), ("img", fellows)))

    def columns(ref, fellow, count):
        return ref.at[:, pl.ds(pl.multiple_of(fellow * count, LANES), count)]

    mine = columns(r_ref, my_fellow, wide)
    row_copies = []
    ref_copies = []
    image_copies = []
    for step in range(1, fellows):
        peer = lax.rem(my_fellow + step, fellows)
        row_copies.append(remote(t_ref, tall.at[my_fellow], ts.at[step], tr.at[step], "img", peer))
        image_copies.append(
            remote(
                columns(c_ref, peer, thin), call.at[my_fellow], cs.at[step], cr.at[step], "img", peer
            )
        )
        image_copies.append(
            remote(
                columns(w_ref, peer, wide), wall.at[my_fellow], ws.at[step], wr.at[step], "img", peer
            )
        )
    for step in range(1, owners):
        peer = lax.rem(my_owner + step, owners)
        ref_copies.append(remote(mine, rall.at[my_owner], rs.at[step], rr.at[step], "cls", peer))
    own_copies = [
        pltpu.make_async_copy(place_hbm, place_ref, own_sem.at[5]),
        pltpu.make_async_copy(place_hbm, place_out, own_sem.at[6]),
        pltpu.make_async_copy(sigma_hbm, sigma_ref, own_sem.at[7]),
        pltpu.make_async_copy(fw_hbm, fw_ref, own_sem.at[8]),
        pltpu.make_async_copy(fr_hbm, fr_ref, own_sem.at[9]),
        pltpu.make_async_copy(fp_hbm, fp_ref, own_sem.at[10]),
        pltpu.make_async_copy(back_hbm, back_ref, own_sem.at[11]),
        pltpu.make_async_copy(t_ref, tall.at[my_fellow], own_sem.at[0]),
        pltpu.make_async_copy(columns(c_ref, my_fellow, thin), call.at[my_fellow], own_sem.at[1]),
        pltpu.make_async_copy(columns(w_ref, my_fellow, wide), wall.at[my_fellow], own_sem.at[2]),
        pltpu.make_async_copy(mine, rall.at[my_owner], own_sem.at[3]),
    ]
    for copy in own_copies:
        copy.start()
    arrive()
    for copy in row_copies + ref_copies + image_copies:
        copy.start()
    for copy in own_copies:
        copy.wait()

    inverses = [
        1.0 / jnp.full((particles, LANES), sigma_ref[my_fellow * half + s], F32) for s in range(half)
    ]

    flat_real = real.reshape(owners * per_owner * rows, LANES)
    flat_imag = imag.reshape(owners * per_owner * rows, LANES)

    def transform(blocks, table):
        x = jnp.concatenate(blocks, axis=0).astype(BF16)
        return jnp.dot(x, table, preferred_element_type=F32)

    def place(fellow):
        num = tiles_of(wall[fellow])
        den = tiles_of(call[fellow])
        weighted = []
        power = []
        for s in range(half):
            ctf = piece(den, s * angles, angles)
            scale = ctf * inverses[s]
            power.append(ctf * scale)
            for p in range(2):
                weighted.append(piece(num, (2 * s + p) * angles, angles) * scale)
        hat = transform(weighted + power, fw_ref[...])
        hat = hat[:, :LANES] + hat[:, LANES:]
        for row in range(rows):
            what[pl.ds(fellow * (particles * rows) + row, particles, stride=rows)] = hat[
                row * particles : (row + 1) * particles
            ]

    def tabulate(owner):
        ref = tiles_of(rall[owner])
        given = []
        power = []
        for s in range(half):
            pair = [piece(ref, (2 * s + p) * angles, angles) for p in range(2)]
            given += pair
            squares = pair[0] * pair[0] + pair[1] * pair[1]
            power.append(squares.astype(BF16).astype(F32) * -0.5)
        tall_rows = round_up(per_owner, 8)
        blocks = [
            jnp.concatenate([x, jnp.zeros((tall_rows - per_owner, LANES), F32)], axis=0)
            for x in given + power
        ]
        hat = transform(blocks, fr_ref[...])
        for row in range(rows):
            at = pl.ds(owner * (per_owner * rows) + row, per_owner, stride=rows)
            block = hat[row * tall_rows : row * tall_rows + per_owner]
            flat_real[at] = block[:, :LANES] + block[:, LANES : 2 * LANES]
            flat_imag[at] = block[:, 2 * LANES : 3 * LANES] + block[:, 3 * LANES :]

    place(my_fellow)
    tabulate(my_owner)
    for copy in row_copies:
        copy.wait_recv()
    to_smem = pltpu.make_async_copy(tall, rows_ref, own_sem.at[4])
    to_smem.start()
    for step in range(1, max(owners, fellows)):
        if step < fellows:
            image_copies[2 * step - 2].wait_recv()
            image_copies[2 * step - 1].wait_recv()
            place(lax.rem(my_fellow + fellows - step, fellows))
        if step < owners:
            ref_copies[step - 1].wait_recv()
            tabulate(lax.rem(my_owner + owners - step, owners))
    to_smem.wait()

    batch = 4

    def score(fellow):
        def some(b, carry):
            sums = []
            for k in range(batch):
                i = b * batch + k
                base = pl.multiple_of((fellow * particles + i) * rows, 8)
                held = what[pl.ds(base, rows)]
                for j in range(top):
                    row = place_ref[rows_ref[fellow, j, i]]
                    first = held * real[row]
                    second = held * imag[row]
                    first = jnp.sum(first.reshape(rows // 8, 8, LANES), axis=0)
                    second = jnp.sum(second.reshape(rows // 8, 8, LANES), axis=0)
                    sums.append(jnp.sum(first + roll(second, IMAG), axis=0, keepdims=True))
            count = batch * top
            parts[fellow, pl.ds(pl.multiple_of(b * count, count), count)] = jnp.concatenate(
                sums, axis=0
            )
            return carry

        lax.fori_loop(0, particles // batch, some, 0)

    part_copies = []
    for step in range(1, fellows):
        peer = lax.rem(my_fellow + fellows - step, fellows)
        score(peer)
        copy = remote(
            parts.at[peer], landed.at[step - 1], ls.at[step], lr.at[step], "img", peer
        )
        copy.start()
        part_copies.append(copy)
    score(my_fellow)
    total = parts[my_fellow]
    for step in range(1, fellows):
        part_copies[step - 1].wait_recv()
        total = total + landed[step - 1]
    logits = jnp.dot(
        total, back_ref[...], precision=lax.Precision.HIGHEST, preferred_element_type=F32
    )
    inside = lane_of(logits.shape) < angles
    highest = jnp.max(jnp.where(inside, logits, -jnp.inf), axis=1, keepdims=True)
    highest = group_of(jnp.broadcast_to(highest, logits.shape), top, jnp.maximum)
    exponent = jnp.where(inside, jnp.exp(logits - highest), 0.0)
    summed = jnp.sum(exponent, axis=1, keepdims=True)
    summed = group_of(jnp.broadcast_to(summed, logits.shape), top, jnp.add)
    post[my_fellow] = (exponent / summed).astype(BF16)
    post_copies = []
    for step in range(1, fellows):
        peer = lax.rem(my_fellow + step, fellows)
        at = post.at[my_fellow]
        copy = remote(at, at, ps.at[step], pr.at[step], "img", peer)
        copy.start()
        post_copies.append(copy)
    for copy in row_copies + ref_copies + image_copies + part_copies:
        copy.wait_send()
    for copy in post_copies:
        copy.wait()
    hat = jnp.dot(
        post[...].reshape(fellows * entries, LANES), fp_ref[...], preferred_element_type=F32
    )
    post_real[...] = hat[:, :LANES] + hat[:, LANES : 2 * LANES]
    post_imag[...] = hat[:, 2 * LANES : 3 * LANES] + hat[:, 3 * LANES :]


def total_kernel(dims, place_ref, rows_ref, what, real, imag, acc):
    fellows, particles, owners, per_owner, top, angles, half = dims
    rows = 3 * half
    acc[...] = jnp.zeros_like(acc)
    batch = 4

    def one(fellow, i):
        at = fellow * particles + i
        held = what[pl.ds(pl.multiple_of(at * rows, 8), rows)]
        swapped = roll(held, IMAG)
        spots = [
            pl.ds(pl.multiple_of(place_ref[rows_ref[fellow, j, i]] * rows, 8), rows)
            for j in range(top)
        ]
        before = [acc[spot] for spot in spots]
        for j in range(top):
            e = at * top + j
            acc[spots[j]] = before[j] + held * real[pl.ds(e, 1)] + swapped * imag[pl.ds(e, 1)]

    def some(b, carry):
        for k in range(batch):
            one(b // (particles // batch), lax.rem(b, particles // batch) * batch + k)
        return carry

    lax.fori_loop(0, fellows * particles // batch, some, 0)


def gather_kernel(dims, acc, high_ref, low_ref, out_ref, outbox, landed, flat, send, recv):
    fellows, particles, owners, per_owner, top, angles, half = dims
    rows = 3 * half
    lanes = outbox.shape[2]
    me = lax.axis_index("cls")
    arrive = hail((("cls", owners),))

    def sums(owner):
        x = acc[pl.ds(pl.multiple_of(owner * (per_owner * rows), 8), lanes)]
        high = x.astype(BF16)
        low = (x - high.astype(F32)).astype(BF16)

        def turned(a, b):
            return lax.dot_general(a, b, LAST, preferred_element_type=F32)

        return turned(high_ref[...], high) + (
            turned(high_ref[...], low) + turned(low_ref[...], high)
        )

    copies = []
    for step in range(1, owners):
        peer = lax.rem(me + step, owners)
        outbox[peer] = sums(peer)[:angles].astype(BF16)
        copies.append(
            remote(outbox.at[peer], landed.at[step - 1], send.at[step], recv.at[step], "cls", peer)
        )
        if step == 2:
            arrive()
            copies[0].start()
        if step >= 2:
            copies[-1].start()
    total = sums(me)[:angles]
    for step in range(1, owners):
        copies[step - 1].wait_recv()
        total = total + landed[step - 1].astype(F32)
    total = jnp.concatenate([total, jnp.zeros((LANES - angles, lanes), F32)], axis=0)
    for begin in range(0, lanes, LANES):
        flat[begin : begin + LANES] = total[:, begin : begin + LANES].T
    count = out_ref.shape[1] // LANES
    tiles = [jnp.zeros((per_owner, LANES), F32) for _ in range(count)]
    lane = lane_of((per_owner, LANES))
    for s in range(half):
        den = flat[pl.ds(2 * half + s, per_owner, stride=rows)] + 1.0
        for p in range(2):
            new = flat[pl.ds(2 * s + p, per_owner, stride=rows)] / den
            tile, offset = divmod((2 * s + p) * angles, LANES)
            new = roll(new, offset) if offset else new
            within = (lane >= offset) & (lane < offset + angles)
            tiles[tile] = jnp.where(within, new, tiles[tile])
            if offset + angles > LANES:
                tiles[tile + 1] = jnp.where(lane < offset + angles - LANES, new, tiles[tile + 1])
    for tile, value in enumerate(tiles):
        out_ref[:, tile * LANES : (tile + 1) * LANES] = value
    for copy in copies:
        copy.wait_send()


def spaced(x, fellows):
    count = x.shape[1] // fellows
    wanted = round_up(count, LANES)
    if wanted == count:
        return x, count
    x = jnp.pad(x.reshape(x.shape[0], fellows, count), ((0, 0), (0, 0), (0, wanted - count)))
    return x.reshape(x.shape[0], fellows * wanted), wanted


def on_device(images, ctf, classes, class_place, references, sigma2):
    shells = sigma2.shape[0]
    angles = ctf.shape[1] // shells
    particles = images.shape[0]
    per_owner = references.shape[0]
    top = classes.shape[1]
    owners = lax.axis_size("cls")
    fellows = lax.axis_size("img")
    half = shells // fellows
    rows = 3 * half
    dims = (fellows, particles, owners, per_owner, top, angles, half)
    everyone = fellows * particles
    total = owners * per_owner
    lanes = round_up(per_owner * rows, LANES)
    acc_rows = round_up((total - per_owner) * rows + lanes, 8)

    images, wide = spaced(images, fellows)
    ctf, thin = spaced(ctf, fellows)
    references, _ = spaced(references, fellows)

    cos, sin, back = waves(angles)
    both = np.concatenate([cos, cos], axis=1)
    forward = jnp.asarray(paired(np.concatenate([cos, -sin], axis=1)))
    of_refs = jnp.asarray(paired(both, np.concatenate([sin, -sin], axis=1)))
    of_post = jnp.asarray(paired(both, np.concatenate([-sin, sin], axis=1)))
    back_high, back_low = halves(back[: round_up(angles, 16)])
    smem = pl.BlockSpec(memory_space=pltpu.SMEM)
    dma = pltpu.SemaphoreType.DMA
    what, real, imag, tall, placed = pl.pallas_call(
        functools.partial(score_kernel, dims),
        out_shape=(
            jax.ShapeDtypeStruct((everyone * rows, LANES), F32),
            jax.ShapeDtypeStruct((everyone * top, LANES), F32),
            jax.ShapeDtypeStruct((everyone * top, LANES), F32),
            jax.ShapeDtypeStruct((fellows, top, particles), jnp.int32),
            jax.ShapeDtypeStruct((total,), jnp.int32),
        ),
        in_specs=specs(10, pltpu.HBM),
        out_specs=tuple(specs(5)),
        scratch_shapes=[
            pltpu.SMEM((total,), jnp.int32),
            pltpu.SMEM((shells,), F32),
            VMEM(forward.shape, BF16),
            VMEM(of_refs.shape, BF16),
            VMEM(of_post.shape, BF16),
            VMEM(back.shape, F32),
            VMEM((fellows, particles * top, LANES), BF16),
            VMEM((fellows, particles, wide), BF16),
            VMEM((fellows, particles, thin), BF16),
            VMEM((owners, per_owner, wide), BF16),
            pltpu.SMEM((fellows, top, particles), jnp.int32),
            VMEM((total, rows, LANES), F32),
            VMEM((total, rows, LANES), F32),
            VMEM((fellows, particles * top, LANES), F32),
            VMEM((fellows - 1, particles * top, LANES), F32),
            dma((12,)),
            dma((fellows,)),
            dma((fellows,)),
            dma((fellows,)),
            dma((fellows,)),
            dma((owners,)),
            dma((owners,)),
            dma((fellows,)),
            dma((fellows,)),
            dma((fellows,)),
            dma((fellows,)),
            dma((fellows,)),
            dma((fellows,)),
        ],
        compiler_params=pltpu.CompilerParams(
            collective_id=0, has_side_effects=True, vmem_limit_bytes=WIDE
        ),
    )(
        class_place, sigma2, images, ctf, references, classes.T,
        forward, of_refs, of_post, jnp.asarray(back.T, F32),
    )
    acc = pl.pallas_call(
        functools.partial(total_kernel, dims),
        out_shape=jax.ShapeDtypeStruct((acc_rows, LANES), F32),
        in_specs=[smem, smem] + specs(3),
        out_specs=specs(1)[0],
        compiler_params=pltpu.CompilerParams(vmem_limit_bytes=WIDE),
    )(placed, tall, what, real, imag)
    return pl.pallas_call(
        functools.partial(gather_kernel, dims),
        out_shape=jax.ShapeDtypeStruct((per_owner, 2 * half * angles), F32),
        in_specs=specs(3),
        out_specs=specs(1)[0],
        scratch_shapes=[
            VMEM((owners, angles, lanes), BF16),
            VMEM((owners - 1, angles, lanes), BF16),
            VMEM((lanes, LANES), F32),
            dma((owners,)),
            dma((owners,)),
        ],
        compiler_params=pltpu.CompilerParams(
            collective_id=2, has_side_effects=True, vmem_limit_bytes=LIMIT
        ),
    )(acc, jnp.asarray(back_high), jnp.asarray(back_low))


def solution(mesh):
    in_specs = (
        P(("cls", "img"), None),
        P(("cls", "img"), None),
        P(("cls", "img"), None),
        P(),
        P("cls", None),
        P(),
    )
    out_specs = P("cls", "img")
    return jax.shard_map(
        on_device, mesh=mesh, in_specs=in_specs, out_specs=out_specs, check_vma=False
    )
```
